256 devices in a mesh: blk: 32 (over x_lo, z, core), cd: 8 (over x_hi, y).
Axes of the slice: x: 4 (x_hi: 2, x_lo: 2; x = x_hi * 2 + x_lo), y: 4, z: 8, core: 2. Of those that a mesh axis runs over, the one named last changes fastest.
Arguments:
- t2_amps: bfloat16 [2048, 32768], P('blk', 'cd'), may hold values from -6 to 6
- integrals: bfloat16 [1024, 64, 4096], P('blk', None, 'cd'), may hold values from -0.09375 to 0.09375
- ab_sym: int32 [1024], P('blk'), may hold values from 0 to 7, as said below
- cd_sym: int32 [512], P('cd'), may hold values from 0 to 7, as said below
Outputs:
- ladder: bfloat16 [2048, 65536], P('cd', 'blk')
The draws below stay inside these ranges and needn't reach their ends.
Inputs may be any that keep to these rules, and one draw needn't show every extreme that they name: `ab_sym`: each aligned block of 32 ab tiles (the tiles of one index of blk) holds exactly 4 tiles of every irreducible representation. `cd_sym`: each group of 64 consecutive cd tiles holds exactly 8 tiles of every irreducible representation.
All inputs are finite; a program needn't handle non-finite values.
Results may differ from the reference program's by a relative error of at most 0.015.
Values may be sent and summed in bfloat16 or wider, within the bound.
A program may use at most 128 MiB of HBM per device.

```python
import jax
import jax.numpy as jnp
from jax import lax

TILE = 64
NSYM = 8
NA_DEV = 32
CT_DEV = 64
KC = 512
NIJ = 2048
NA = 1024
NC = 512
N_CD = 8


def balanced_labels(key, blocks, per_block):
    base = jnp.tile(jnp.arange(NSYM, dtype=jnp.int32), per_block // NSYM)
    keys = jax.random.split(key, blocks)
    rows = jax.vmap(lambda k: jax.random.permutation(k, base))(keys)
    return rows.reshape(blocks * per_block).astype(jnp.int32)


def draw_ab_sym(key, part):
    return balanced_labels(jax.random.fold_in(key, 11), NA // NA_DEV, NA_DEV)


def draw_cd_sym(key, part):
    return balanced_labels(jax.random.fold_in(key, 23), NC // CT_DEV, CT_DEV)


def steps_of(rng, dims, pieces, least, high):
    def one(dim, blocks):
        draws = jax.random.uniform(jax.random.fold_in(jax.random.fold_in(rng, 6), dim), (blocks,), jnp.float32, least / len(pieces), high / len(pieces))
        return jnp.repeat(jnp.exp(draws), dims[dim] // blocks).reshape((-1,) + (1,) * (len(dims) - dim - 1))

    loudness = one(*pieces[0])
    for cut in pieces[1:]:
        loudness = loudness * one(*cut)
    return loudness


def scatter_about(rng, extent, width, most, pieces=(), kind=jnp.bfloat16):
    loudness = steps_of(rng, extent, pieces, -0.22, 0.18) if pieces else 1.0
    entries = jax.random.normal(rng, extent, jnp.float32) * width * loudness
    return jnp.minimum(jnp.maximum(entries, -most), most).astype(kind)


def setup_inputs(seed: int = 0) -> dict:
    key_list = jax.random.split(jax.random.key(seed), 5)
    return {
        "t2_amps": scatter_about(key_list[0], (NIJ, NC * TILE), 1.0, 6.0, ((0, 32), (1, 8))),
        "integrals": scatter_about(key_list[1], (NA, TILE, N_CD * KC), (N_CD * KC) ** -0.5, 0.09375, ((0, 32), (2, 8))),
        "ab_sym": draw_ab_sym(jax.random.fold_in(key_list[4], 71), 0),
        "cd_sym": draw_cd_sym(jax.random.fold_in(key_list[4], 71), 0),
    }


def reference(t2_amps, integrals, ab_sym, cd_sym):
    packed = CT_DEV * TILE // NSYM
    per_sym = NA // NSYM
    order_ab = jnp.argsort(ab_sym, stable=True).astype(jnp.int32)
    inverse_ab = jnp.argsort(order_ab, stable=True).astype(jnp.int32)
    ints_sorted = jnp.take(integrals, order_ab, axis=0).reshape(NSYM, per_sym * TILE, N_CD * packed)

    def group_add(group, acc):
        group = jnp.asarray(group).astype(jnp.int32)
        cd_local = lax.dynamic_slice_in_dim(cd_sym, group * CT_DEV, CT_DEV, 0)
        order_cd = jnp.argsort(cd_local, stable=True).astype(jnp.int32)
        amp_part = lax.dynamic_slice_in_dim(t2_amps, group * (CT_DEV * TILE), CT_DEV * TILE, 1)
        amp_part = jnp.take(amp_part.reshape(NIJ, CT_DEV, TILE), order_cd, axis=1)
        amp_part = amp_part.reshape(NIJ, NSYM, packed).astype(jnp.float32)
        int_part = lax.dynamic_slice_in_dim(ints_sorted, group * packed, packed, 2).astype(jnp.float32)
        partial_value = jnp.einsum("isk,smk->ism", amp_part, int_part)
        rounded = lax.optimization_barrier(partial_value.astype(jnp.bfloat16))
        return acc + rounded.astype(jnp.float32)

    start = jnp.zeros((NIJ, NSYM, per_sym * TILE), jnp.float32)
    total = lax.fori_loop(0, N_CD, group_add, start)
    total = jnp.take(total.reshape(NIJ, NA, TILE), inverse_ab, axis=1)
    return total.reshape(NIJ, NA * TILE).astype(jnp.bfloat16)
```

```python
import jax
import jax.numpy as jnp
from jax import lax
from jax.experimental import pallas as pl
from jax.experimental.pallas import tpu as pltpu
from jax.sharding import PartitionSpec as P

MESH = pl.DeviceIdType.MESH
NSYM = 8
NZ = 8
NY = 4
ROWS = 64
K = 512
SLOT_K = (3, 1, 4, 2)
SLOT_BACK = (1, 0, 1, 0)
LAG2, LAG3, LAG4 = 2, 5, 7


def kernel(
    t2_ref, ints_ref, out_ref,
    gathered, weights, partial, full_hi, full_lo, half_hi, half_lo,
    xsend, xrecv, sib_send, result,
    local_sem, w_s, w_r, x0_s, x0_r, z_s, z_r, yh_s, yh_r, yf_s, yf_r, xh_s, xh_r, co_s, co_r,
):
    blk = lax.axis_index("blk")
    cd = lax.axis_index("cd")
    core = lax.rem(blk, 2)
    z = lax.rem(blk // 2, NZ)
    xl = blk // (2 * NZ)
    y = lax.rem(cd, NY)
    xh = cd // NY

    def dev(xl_, z_, core_, xh_, y_):
        return ((xl_ * NZ + z_) * 2 + core_, xh_ * NY + y_)

    def zmod(v):
        return lax.rem(v + 2 * NZ, NZ)

    def ymod(v):
        return lax.rem(v + 2 * NY, NY)

    z_dev = (dev(xl, zmod(z + 1), core, xh, y), dev(xl, zmod(z - 1), core, xh, y))
    x_dev = dev(1 - xl, z, core, xh, y)
    yp_dev = dev(xl, z, core, xh, ymod(y + 1))
    ym_dev = dev(xl, z, core, xh, ymod(y - 1))
    xh_dev = dev(xl, z, core, 1 - xh, y)
    co_dev = dev(xl, z, 1 - core, xh, y)

    def remote(src, dst, send, recv, device):
        return pltpu.make_async_remote_copy(
            src_ref=src, dst_ref=dst, send_sem=send, recv_sem=recv,
            device_id=device, device_id_type=MESH,
        )

    t2_copy = pltpu.make_async_copy(t2_ref, gathered.at[:, z, xl], local_sem.at[0])
    t2_copy.start()
    ints_copy = pltpu.make_async_copy(ints_ref, weights.at[:, pl.ds(0, 256)], local_sem.at[1])
    ints_copy.start()

    barrier = pltpu.get_barrier_semaphore()
    for device in (z_dev[0], z_dev[1], x_dev, yp_dev, ym_dev, xh_dev, co_dev):
        pl.semaphore_signal(barrier, inc=1, device_id=device, device_id_type=MESH)
    pl.semaphore_wait(barrier, 7)

    def x0_copy(s, col):
        return remote(t2_ref.at[s], gathered.at[s, z, col], x0_s.at[s], x0_r.at[s], x_dev)

    def w_copy(s):
        return remote(
            ints_ref.at[s], weights.at[s, pl.ds(256, 256)], w_s.at[s], w_r.at[s], co_dev
        )

    def send_own(s, carry):
        x0_copy(s, xl).start()
        w_copy(s).start()
        return carry

    lax.fori_loop(0, NSYM, send_own, 0)
    t2_copy.wait()
    ints_copy.wait()

    def z_copy(s, k, direction, sender_side):
        sign = -1 if direction == 0 else 1
        b = zmod(z + sign * (k - 1 if sender_side else k))
        view = gathered.at[s, b] if k < 4 else gathered.at[s, b, direction]
        return remote(view, view, z_s.at[k - 1, direction, s], z_r.at[k - 1, direction, s], z_dev[direction])

    def z_send(s, k):
        for direction in range(2):
            z_copy(s, k, direction, True).start()

    def z_recv(s, k):
        for direction in range(2):
            z_copy(s, k, direction, False).wait_recv()

    turn = jnp.where(lax.rem(z, 2) == 0, -1, 1)

    def owner(k):
        own = z // 2
        return ymod((own, own + turn, own - turn, own + 2)[k - 1])

    def half_copy(s, k, side):
        if side == 0:
            return remote(partial.at[s, k - 1, 0], half_hi.at[s], yh_s.at[0, s], yh_r.at[0, s], ym_dev)
        return remote(partial.at[s, k - 1, 1], half_lo.at[s], yh_s.at[1, s], yh_r.at[1, s], yp_dev)

    def full_copy(s, k, side):
        if side == 0:
            return remote(partial.at[s, k - 1], full_hi.at[s], yf_s.at[0, s], yf_r.at[0, s], ym_dev)
        return remote(partial.at[s, k - 1], full_lo.at[s], yf_s.at[1, s], yf_r.at[1, s], yp_dev)

    def xh_copy(s):
        return remote(xsend.at[s], xrecv.at[s], xh_s.at[s], xh_r.at[s], xh_dev)

    def co_copy(s, whose):
        return remote(
            sib_send.at[s], result.at[pl.ds(2 * s, 2), :, whose], co_s.at[s], co_r.at[s], co_dev
        )

    def stage1(s, k):
        first = 2 * owner(k)
        rows = gathered[s, pl.ds(first, 2)].reshape(4 * ROWS, K)
        product = lax.dot_general(
            rows, weights[s], (((1,), (1,)), ((), ())), preferred_element_type=jnp.float32
        )
        partial[s, k - 1] = product.astype(jnp.bfloat16).reshape(2, 2, ROWS, 512)

        @pl.when(ymod(y - owner(k)) == 2)
        def _():
            half_copy(s, k, 0).start()
            half_copy(s, k, 1).start()

    def stage2(s, k):
        d = ymod(y - owner(k))
        for side, role, recv in ((0, 1, half_hi), (1, 3, half_lo)):
            @pl.when(d == role)
            def _():
                half_copy(s, k, side).wait_recv()
                partial[s, k - 1, side] = (
                    partial[s, k - 1, side].astype(jnp.float32) + recv[s].astype(jnp.float32)
                ).astype(jnp.bfloat16)
                full_copy(s, k, side).start()

    def three(s, k, col):
        return (
            partial[s, k - 1, :, col].astype(jnp.float32)
            + full_hi[s, :, col].astype(jnp.float32)
            + full_lo[s, :, col].astype(jnp.float32)
        )

    def stage3(s, k):
        @pl.when(y == owner(k))
        def _():
            full_copy(s, k, 0).wait_recv()
            full_copy(s, k, 1).wait_recv()
            xsend[s] = three(s, k, 1 - xh).astype(jnp.bfloat16)
            xh_copy(s).start()

    def stage4(s, k):
        @pl.when(y == owner(k))
        def _():
            xh_copy(s).wait_recv()
            final = (three(s, k, xh) + xrecv[s].astype(jnp.float32)).astype(jnp.bfloat16)
            for h in range(2):
                result[2 * s + h, :, core] = final[:, :, 128 * h:128 * (h + 1)]
                sib_send[s, h] = final[:, :, 256 + 128 * h:256 + 128 * (h + 1)]
            co_copy(s, core).start()

    def when_valid(s, act):
        @pl.when(jnp.logical_and(s >= 0, s < NSYM))
        def _():
            act()

    def lagged(tick, slot, lag, stage):
        q = slot - lag
        j, back = q % 4, q // 4
        s = tick + back - SLOT_BACK[j]
        when_valid(s, lambda: stage(s, SLOT_K[j]))

    def tick_body(tick, carry):
        def begin():
            x0_copy(tick, 1 - xl).wait_recv()
            z_send(tick, 1)

        when_valid(tick, begin)
        for slot in range(4):
            k, s = SLOT_K[slot], tick - SLOT_BACK[slot]

            def arrive(k=k, s=s):
                z_recv(s, k)
                if k < 4:
                    z_send(s, k + 1)
                if k == 1:
                    w_copy(s).wait_recv()
                stage1(s, k)

            when_valid(s, arrive)
            lagged(tick, slot, LAG2, stage2)
            lagged(tick, slot, LAG3, stage3)
            lagged(tick, slot, LAG4, stage4)
        return carry

    lax.fori_loop(0, NSYM + 1 + (LAG4 + 3) // 4, tick_body, 0)

    def drain(s, carry):
        x0_copy(s, xl).wait_send()
        w_copy(s).wait_send()
        for k in range(1, 5):
            for direction in range(2):
                z_copy(s, k, direction, True).wait_send()
        for side in range(2):
            half_copy(s, 1, side).wait_send()
            full_copy(s, 1, side).wait_send()
        xh_copy(s).wait_send()
        co_copy(s, core).wait_send()
        co_copy(s, 1 - core).wait_recv()
        return carry

    lax.fori_loop(0, NSYM, drain, 0)

    out_copy = pltpu.make_async_copy(result, out_ref, local_sem.at[0])
    out_copy.start()
    out_copy.wait()


def merge_tiles(load, first, second):
    pieces = []
    for want, tile in ((0, first), (1, second)):
        a = load(tile // 2).astype(jnp.float32)
        pieces.append(jnp.where(lax.rem(tile, 2) == want, a, pltpu.roll(a, 64, 1)))
    lane = lax.broadcasted_iota(jnp.int32, pieces[0].shape, 1)
    return jnp.where(lane < 64, pieces[0], pieces[1]).astype(jnp.bfloat16)


def sort_kernel(ab_ref, cd_ref, t2_ref, ints_ref, t2_out, ints_out, inverse_ref, order, count):
    def clear(s, carry):
        count[s] = 0
        count[NSYM + s] = 0
        return carry

    lax.fori_loop(0, NSYM, clear, 0)

    def place_cd(i, carry):
        s = cd_ref[i]
        c = count[s]
        order[s * 8 + c] = i
        count[s] = c + 1
        return carry

    lax.fori_loop(0, 64, place_cd, 0)

    def place_ab(i, carry):
        s = ab_ref[i]
        c = count[NSYM + s]
        inverse_ref[i] = s * 4 + c
        ints_out[s, pl.ds(pl.multiple_of(c * 64, 64), 64)] = ints_ref[i]
        count[NSYM + s] = c + 1
        return carry

    lax.fori_loop(0, 32, place_ab, 0)

    def load(chunk):
        return t2_ref[:, pl.ds(pl.multiple_of(chunk * 128, 128), 128)]

    def sort_t2(s, carry):
        for j in range(K // 128):
            t2_out[s, :, 128 * j:128 * (j + 1)] = merge_tiles(
                load, order[s * 8 + 2 * j], order[s * 8 + 2 * j + 1]
            )
        return carry

    lax.fori_loop(0, NSYM, sort_t2, 0)


def unsort_kernel(inverse_ref, sorted_ref, out_ref):
    for p in range(16):
        out_ref[:, 128 * p:128 * (p + 1)] = merge_tiles(
            lambda chunk: sorted_ref[chunk], inverse_ref[2 * p], inverse_ref[2 * p + 1]
        )


def per_device(t2_amps, integrals, ab_sym, cd_sym):
    bf16 = jnp.bfloat16
    dma = pltpu.SemaphoreType.DMA
    smem = pl.BlockSpec(memory_space=pltpu.SMEM)
    vmem = pl.BlockSpec(memory_space=pltpu.VMEM)
    t2_sorted, ints_sorted, inverse = pl.pallas_call(
        sort_kernel,
        out_shape=(
            jax.ShapeDtypeStruct((NSYM, ROWS, K), bf16),
            jax.ShapeDtypeStruct((NSYM, 256, K), bf16),
            jax.ShapeDtypeStruct((32,), jnp.int32),
        ),
        in_specs=[smem, smem, vmem, vmem],
        out_specs=(vmem, vmem, smem),
        scratch_shapes=[pltpu.SMEM((64,), jnp.int32), pltpu.SMEM((16,), jnp.int32)],
    )(ab_sym, cd_sym, t2_amps, integrals)
    result = pl.pallas_call(
        kernel,
        out_shape=jax.ShapeDtypeStruct((2 * NSYM, 2, 2, ROWS, 128), bf16),
        in_specs=[
            pl.BlockSpec(memory_space=pl.ANY),
            pl.BlockSpec(memory_space=pl.ANY),
        ],
        out_specs=pl.BlockSpec(memory_space=pl.ANY),
        scratch_shapes=[
            pltpu.VMEM((NSYM, NZ, 2, ROWS, K), bf16),
            pltpu.VMEM((NSYM, 512, K), bf16),
            pltpu.VMEM((NSYM, 4, 2, 2, ROWS, 512), bf16),
            pltpu.VMEM((NSYM, 2, 2, ROWS, 512), bf16),
            pltpu.VMEM((NSYM, 2, 2, ROWS, 512), bf16),
            pltpu.VMEM((NSYM, 2, ROWS, 512), bf16),
            pltpu.VMEM((NSYM, 2, ROWS, 512), bf16),
            pltpu.VMEM((NSYM, 2, ROWS, 512), bf16),
            pltpu.VMEM((NSYM, 2, ROWS, 512), bf16),
            pltpu.VMEM((NSYM, 2, 2, ROWS, 128), bf16),
            pltpu.VMEM((2 * NSYM, 2, 2, ROWS, 128), bf16),
            dma((2,)),
            dma((NSYM,)), dma((NSYM,)),
            dma((NSYM,)), dma((NSYM,)),
            dma((4, 2, NSYM)), dma((4, 2, NSYM)),
            dma((2, NSYM)), dma((2, NSYM)),
            dma((2, NSYM)), dma((2, NSYM)),
            dma((NSYM,)), dma((NSYM,)),
            dma((NSYM,)), dma((NSYM,)),
        ],
        compiler_params=pltpu.CompilerParams(
            collective_id=0, has_side_effects=True, vmem_limit_bytes=40 << 20
        ),
    )(t2_sorted, ints_sorted)
    return pl.pallas_call(
        unsort_kernel,
        out_shape=jax.ShapeDtypeStruct((256, 2048), bf16),
        in_specs=[smem, vmem],
        out_specs=vmem,
    )(inverse, result.reshape(2 * NSYM, 256, 128))


def solution(mesh):
    in_specs = (P("blk", "cd"), P("blk", None, "cd"), P("blk"), P("cd"))
    out_specs = P("cd", "blk")
    return jax.shard_map(
        per_device, mesh=mesh, in_specs=in_specs, out_specs=out_specs, check_vma=False
    )
```

```python
import jax
import jax.numpy as jnp
from jax import lax
from jax.experimental import pallas as pl
from jax.experimental.pallas import tpu as pltpu
from jax.sharding import PartitionSpec as P

MESH = pl.DeviceIdType.MESH
NSYM = 8
NZ = 8
NY = 4
ROWS = 64
K = 512
SLOT_K = (2, 3, 1, 4)
SLOT_BACK = (1, 2, 0, 2)
LAG2, LAG3, LAG4 = 3, 7, 10


def kernel(
    t2_ref, ints_ref, out_ref,
    gathered, weights, partial, full_hi, full_lo, half_hi, half_lo,
    xsend, xrecv, sib_send, result,
    local_sem, w_s, w_r, x0_s, x0_r, z_s, z_r, xf_s, xf_r, yh_s, yh_r, yf_s, yf_r, xh_s, xh_r, co_s, co_r,
):
    blk = lax.axis_index("blk")
    cd = lax.axis_index("cd")
    core = lax.rem(blk, 2)
    z = lax.rem(blk // 2, NZ)
    xl = blk // (2 * NZ)
    y = lax.rem(cd, NY)
    xh = cd // NY

    def dev(xl_, z_, core_, xh_, y_):
        return ((xl_ * NZ + z_) * 2 + core_, xh_ * NY + y_)

    def zmod(v):
        return lax.rem(v + 2 * NZ, NZ)

    def ymod(v):
        return lax.rem(v + 2 * NY, NY)

    z_dev = (dev(xl, zmod(z + 1), core, xh, y), dev(xl, zmod(z - 1), core, xh, y))
    x_dev = dev(1 - xl, z, core, xh, y)
    yp_dev = dev(xl, z, core, xh, ymod(y + 1))
    ym_dev = dev(xl, z, core, xh, ymod(y - 1))
    xh_dev = dev(xl, z, core, 1 - xh, y)
    co_dev = dev(xl, z, 1 - core, xh, y)

    def remote(src, dst, send, recv, device):
        return pltpu.make_async_remote_copy(
            src_ref=src, dst_ref=dst, send_sem=send, recv_sem=recv,
            device_id=device, device_id_type=MESH,
        )

    t2_copy = pltpu.make_async_copy(t2_ref, gathered.at[:, z, xl], local_sem.at[0])
    t2_copy.start()
    ints_copy = pltpu.make_async_copy(ints_ref, weights.at[:, pl.ds(0, 256)], local_sem.at[1])
    ints_copy.start()

    barrier = pltpu.get_barrier_semaphore()
    for device in (z_dev[0], z_dev[1], x_dev, yp_dev, ym_dev, xh_dev, co_dev):
        pl.semaphore_signal(barrier, inc=1, device_id=device, device_id_type=MESH)
    pl.semaphore_wait(barrier, 7)

    def x0_copy(s, col):
        return remote(t2_ref.at[s], gathered.at[s, z, col], x0_s.at[s], x0_r.at[s], x_dev)

    def w_copy(s):
        return remote(
            ints_ref.at[s], weights.at[s, pl.ds(256, 256)], w_s.at[s], w_r.at[s], co_dev
        )

    def send_own(s, carry):
        x0_copy(s, xl).start()
        w_copy(s).start()
        return carry

    lax.fori_loop(0, NSYM, send_own, 0)
    t2_copy.wait()
    ints_copy.wait()

    def z_copy(s, k, direction, sender_side):
        sign = -1 if direction == 0 else 1
        b = zmod(z + sign * (k - 1 if sender_side else k))
        if k < 3:
            view = gathered.at[s, b]
        elif k == 3:
            view = gathered.at[s, b, xl]
        else:
            view = gathered.at[s, b, xl, pl.ds(32 * direction, 32)]
        return remote(view, view, z_s.at[k - 1, direction, s], z_r.at[k - 1, direction, s], z_dev[direction])

    def z_send(s, k):
        for direction in range(2):
            z_copy(s, k, direction, True).start()

    def z_recv(s, k):
        for direction in range(2):
            z_copy(s, k, direction, False).wait_recv()

    def xf_copy(s, f, sender_side):
        col = xl if sender_side else 1 - xl
        view = gathered.at[s, zmod(z + (-3, 3, 4)[f]), col]
        return remote(view, view, xf_s.at[f, s], xf_r.at[f, s], x_dev)

    turn = jnp.where(lax.rem(z, 2) == 0, -1, 1)

    def owner(k):
        own = z // 2
        return ymod((own, own + turn, own - turn, own + 2)[k - 1])

    def half_copy(s, k, side):
        if side == 0:
            return remote(partial.at[s, k - 1, 0], half_hi.at[s], yh_s.at[0, s], yh_r.at[0, s], ym_dev)
        return remote(partial.at[s, k - 1, 1], half_lo.at[s], yh_s.at[1, s], yh_r.at[1, s], yp_dev)

    def full_copy(s, k, side):
        if side == 0:
            return remote(partial.at[s, k - 1], full_hi.at[s], yf_s.at[0, s], yf_r.at[0, s], ym_dev)
        return remote(partial.at[s, k - 1], full_lo.at[s], yf_s.at[1, s], yf_r.at[1, s], yp_dev)

    def xh_copy(s):
        return remote(xsend.at[s], xrecv.at[s], xh_s.at[s], xh_r.at[s], xh_dev)

    def co_copy(s, whose):
        return remote(
            sib_send.at[s], result.at[pl.ds(2 * s, 2), :, whose], co_s.at[s], co_r.at[s], co_dev
        )

    def stage1(s, k):
        first = 2 * owner(k)
        rows = gathered[s, pl.ds(first, 2)].reshape(4 * ROWS, K)
        product = lax.dot_general(
            rows, weights[s], (((1,), (1,)), ((), ())), preferred_element_type=jnp.float32
        )
        partial[s, k - 1] = product.astype(jnp.bfloat16).reshape(2, 2, ROWS, 512)

        @pl.when(ymod(y - owner(k)) == 2)
        def _():
            half_copy(s, k, 0).start()
            half_copy(s, k, 1).start()

    def stage2(s, k):
        d = ymod(y - owner(k))
        for side, role, recv in ((0, 1, half_hi), (1, 3, half_lo)):
            @pl.when(d == role)
            def _():
                half_copy(s, k, side).wait_recv()
                partial[s, k - 1, side] = (
                    partial[s, k - 1, side].astype(jnp.float32) + recv[s].astype(jnp.float32)
                ).astype(jnp.bfloat16)
                full_copy(s, k, side).start()

    def three(s, k, col):
        return (
            partial[s, k - 1, :, col].astype(jnp.float32)
            + full_hi[s, :, col].astype(jnp.float32)
            + full_lo[s, :, col].astype(jnp.float32)
        )

    def stage3(s, k):
        @pl.when(y == owner(k))
        def _():
            full_copy(s, k, 0).wait_recv()
            full_copy(s, k, 1).wait_recv()
            xsend[s] = three(s, k, 1 - xh).astype(jnp.bfloat16)
            xh_copy(s).start()

    def stage4(s, k):
        @pl.when(y == owner(k))
        def _():
            xh_copy(s).wait_recv()
            final = (three(s, k, xh) + xrecv[s].astype(jnp.float32)).astype(jnp.bfloat16)
            for h in range(2):
                result[2 * s + h, :, core] = final[:, :, 128 * h:128 * (h + 1)]
                sib_send[s, h] = final[:, :, 256 + 128 * h:256 + 128 * (h + 1)]
            co_copy(s, core).start()

    def when_valid(s, act):
        @pl.when(jnp.logical_and(s >= 0, s < NSYM))
        def _():
            act()

    def lagged(tick, slot, lag, stage):
        q = slot - lag
        j, back = q % 4, q // 4
        s = tick + back - SLOT_BACK[j]
        when_valid(s, lambda: stage(s, SLOT_K[j]))

    def begin(s):
        x0_copy(s, 1 - xl).wait_recv()
        z_send(s, 1)

    def arrive(s, k):
        z_recv(s, k)
        if k < 4:
            z_send(s, k + 1)
        if k == 3:
            xf_copy(s, 0, True).start()
            xf_copy(s, 1, True).start()
        if k == 4:
            xf_copy(s, 2, True).start()

    def multiply(s, k):
        if k == 1:
            w_copy(s).wait_recv()
        if k == 3:
            xf_copy(s, 0, False).wait_recv()
            xf_copy(s, 1, False).wait_recv()
        if k == 4:
            xf_copy(s, 2, False).wait_recv()
        stage1(s, k)

    def tick_body(tick, carry):
        def run(back, act, *args):
            when_valid(tick - back, lambda: act(tick - back, *args))

        def unit(slot):
            run(SLOT_BACK[slot], multiply, SLOT_K[slot])
            lagged(tick, slot, LAG2, stage2)
            lagged(tick, slot, LAG3, stage3)
            lagged(tick, slot, LAG4, stage4)

        run(0, begin)
        run(2, arrive, 4)
        run(1, arrive, 2)
        unit(0)
        unit(1)
        run(0, arrive, 1)
        unit(2)
        run(1, arrive, 3)
        unit(3)
        return carry

    lax.fori_loop(0, NSYM + 2 + (LAG4 + 3) // 4, tick_body, 0)

    def drain(s, carry):
        x0_copy(s, xl).wait_send()
        w_copy(s).wait_send()
        for k in range(1, 5):
            for direction in range(2):
                z_copy(s, k, direction, True).wait_send()
        for f in range(3):
            xf_copy(s, f, True).wait_send()
        for side in range(2):
            half_copy(s, 1, side).wait_send()
            full_copy(s, 1, side).wait_send()
        xh_copy(s).wait_send()
        co_copy(s, core).wait_send()
        co_copy(s, 1 - core).wait_recv()
        return carry

    lax.fori_loop(0, NSYM, drain, 0)

    out_copy = pltpu.make_async_copy(result, out_ref, local_sem.at[0])
    out_copy.start()
    out_copy.wait()


def merge_tiles(load, first, second):
    pieces = []
    for want, tile in ((0, first), (1, second)):
        a = load(tile // 2)
        pieces.append(jnp.where(lax.rem(tile, 2) == want, a, pltpu.roll(a, 64, 1)))
    lane = lax.broadcasted_iota(jnp.int32, pieces[0].shape, 1)
    return jnp.where(lane < 64, pieces[0], pieces[1])


def sort_kernel(ab_ref, cd_ref, t2_ref, ints_ref, t2_out, ints_out, inverse_ref, order, count, sem):
    def clear(s, carry):
        count[s] = 0
        count[NSYM + s] = 0
        return carry

    lax.fori_loop(0, NSYM, clear, 0)

    def place_cd(i, carry):
        s = cd_ref[i]
        c = count[s]
        order[s * 8 + c] = i
        count[s] = c + 1
        return carry

    lax.fori_loop(0, 64, place_cd, 0)

    def place_ab(i, carry):
        s = ab_ref[i]
        c = count[NSYM + s]
        inverse_ref[i] = s * 4 + c
        pltpu.make_async_copy(ints_ref.at[i], ints_out.at[s, c], sem).start()
        count[NSYM + s] = c + 1
        return carry

    lax.fori_loop(0, 32, place_ab, 0)
    whole = pltpu.make_async_copy(ints_out, ints_out, sem)

    def load(chunk):
        return t2_ref[:, pl.ds(pl.multiple_of(chunk * 128, 128), 128)]

    def sort_t2(s, carry):
        for j in range(K // 128):
            t2_out[s, :, 128 * j:128 * (j + 1)] = merge_tiles(
                load, order[s * 8 + 2 * j], order[s * 8 + 2 * j + 1]
            )
        return carry

    lax.fori_loop(0, NSYM, sort_t2, 0)
    whole.wait()


def unsort_kernel(inverse_ref, sorted_ref, out_ref):
    for p in range(16):
        out_ref[:, 128 * p:128 * (p + 1)] = merge_tiles(
            lambda chunk: sorted_ref[chunk], inverse_ref[2 * p], inverse_ref[2 * p + 1]
        )


def per_device(t2_amps, integrals, ab_sym, cd_sym):
    bf16 = jnp.bfloat16
    dma = pltpu.SemaphoreType.DMA
    smem = pl.BlockSpec(memory_space=pltpu.SMEM)
    vmem = pl.BlockSpec(memory_space=pltpu.VMEM)
    hbm = pl.BlockSpec(memory_space=pltpu.HBM)
    t2_sorted, ints_sorted, inverse = pl.pallas_call(
        sort_kernel,
        out_shape=(
            jax.ShapeDtypeStruct((NSYM, ROWS, K), bf16),
            jax.ShapeDtypeStruct((NSYM, 4, 64, K), bf16),
            jax.ShapeDtypeStruct((32,), jnp.int32),
        ),
        in_specs=[smem, smem, vmem, hbm],
        out_specs=(vmem, vmem, smem),
        scratch_shapes=[pltpu.SMEM((64,), jnp.int32), pltpu.SMEM((16,), jnp.int32), dma(())],
    )(ab_sym, cd_sym, t2_amps, integrals)
    result = pl.pallas_call(
        kernel,
        out_shape=jax.ShapeDtypeStruct((2 * NSYM, 2, 2, ROWS, 128), bf16),
        in_specs=[hbm, hbm],
        out_specs=hbm,
        scratch_shapes=[
            pltpu.VMEM((NSYM, NZ, 2, ROWS, K), bf16),
            pltpu.VMEM((NSYM, 512, K), bf16),
            pltpu.VMEM((NSYM, 4, 2, 2, ROWS, 512), bf16),
            pltpu.VMEM((NSYM, 2, 2, ROWS, 512), bf16),
            pltpu.VMEM((NSYM, 2, 2, ROWS, 512), bf16),
            pltpu.VMEM((NSYM, 2, ROWS, 512), bf16),
            pltpu.VMEM((NSYM, 2, ROWS, 512), bf16),
            pltpu.VMEM((NSYM, 2, ROWS, 512), bf16),
            pltpu.VMEM((NSYM, 2, ROWS, 512), bf16),
            pltpu.VMEM((NSYM, 2, 2, ROWS, 128), bf16),
            pltpu.VMEM((2 * NSYM, 2, 2, ROWS, 128), bf16),
            dma((2,)),
            dma((NSYM,)), dma((NSYM,)),
            dma((NSYM,)), dma((NSYM,)),
            dma((4, 2, NSYM)), dma((4, 2, NSYM)),
            dma((3, NSYM)), dma((3, NSYM)),
            dma((2, NSYM)), dma((2, NSYM)),
            dma((2, NSYM)), dma((2, NSYM)),
            dma((NSYM,)), dma((NSYM,)),
            dma((NSYM,)), dma((NSYM,)),
        ],
        compiler_params=pltpu.CompilerParams(
            collective_id=0, has_side_effects=True, vmem_limit_bytes=62 << 20
        ),
    )(t2_sorted, ints_sorted.reshape(NSYM, 256, K))
    return pl.pallas_call(
        unsort_kernel,
        out_shape=jax.ShapeDtypeStruct((256, 2048), bf16),
        grid=(4,),
        in_specs=[smem, pl.BlockSpec((2 * NSYM, ROWS, 128), lambda i: (0, i, 0))],
        out_specs=pl.BlockSpec((ROWS, 2048), lambda i: (i, 0)),
    )(inverse, result.reshape(2 * NSYM, 256, 128))


def solution(mesh):
    in_specs = (P("blk", "cd"), P("blk", None, "cd"), P("blk"), P("cd"))
    out_specs = P("cd", "blk")
    return jax.shard_map(
        per_device, mesh=mesh, in_specs=in_specs, out_specs=out_specs, check_vma=False
    )
```

```python
import jax
import jax.numpy as jnp
from jax import lax
from jax.experimental import pallas as pl
from jax.experimental.pallas import tpu as pltpu
from jax.sharding import PartitionSpec as P

MESH = pl.DeviceIdType.MESH
NSYM = 8
NZ = 8
NY = 4
ROWS = 64
K = 512
WIDE = 6
NARROW = NSYM - WIDE
EARLY = 2
SCHEDULE = (
    ("begin", 0, 0),
    ("add", 3, 3),
    ("arrive", 2, 1),
    ("arrive", 4, 2),
    ("multiply", 3, 2),
    ("add", 2, 2),
    ("multiply", 2, 1),
    ("finish", 3, 5),
    ("own", 3, 4),
    ("finish", 2, 4),
    ("own", 2, 3),
    ("forward", 0, -2),
    ("arrive", 1, 0),
    ("rows", 0, -6),
    ("add", 1, 1),
    ("add", 4, 3),
    ("arrive", 3, 1),
    ("multiply", 1, 0),
    ("multiply", 4, 2),
    ("weights", 0, -6),
    ("finish", 1, 3),
    ("finish", 4, 5),
    ("own", 1, 2),
    ("own", 4, 4),
    ("first", 1, -2),
)


def kernel(
    t2_ref, ints_ref, out_ref,
    gathered, weights, partial, full_hi, full_lo, half_hi, half_lo, xsend, xrecv,
    n_partial, n_full_hi, n_full_lo, n_half_hi, n_half_lo, n_sib, sib_send, result,
    local_sem, w_s, w_r, x0_s, x0_r, z_s, z_r, xf_s, xf_r, yh_s, yh_r, yf_s, yf_r, xh_s, xh_r,
    co_s, co_r, wx_s, wx_r, wf_s, wf_r, pb_s, pb_r,
):
    blk = lax.axis_index("blk")
    cd = lax.axis_index("cd")
    core = lax.rem(blk, 2)
    z = lax.rem(blk // 2, NZ)
    xl = blk // (2 * NZ)
    y = lax.rem(cd, NY)
    xh = cd // NY

    def dev(xl_, z_, core_, xh_, y_):
        return ((xl_ * NZ + z_) * 2 + core_, xh_ * NY + y_)

    def zmod(v):
        return lax.rem(v + 2 * NZ, NZ)

    def ymod(v):
        return lax.rem(v + 2 * NY, NY)

    z_dev = (dev(xl, zmod(z + 1), core, xh, y), dev(xl, zmod(z - 1), core, xh, y))
    x_dev = dev(1 - xl, z, core, xh, y)
    xh_dev = dev(xl, z, core, 1 - xh, y)
    xd_dev = dev(1 - xl, z, core, 1 - xh, y)
    yp_dev = dev(xl, z, core, xh, ymod(y + 1))
    ym_dev = dev(xl, z, core, xh, ymod(y - 1))
    co_dev = dev(xl, z, 1 - core, xh, y)
    yp_other = dev(xl, z, 1 - core, xh, ymod(y + 1))
    ym_other = dev(xl, z, 1 - core, xh, ymod(y - 1))
    outer = xl == xh
    inner = jnp.logical_not(outer)
    wide, narrow = pl.ds(0, WIDE), pl.ds(WIDE, NARROW)

    def remote(src, dst, send, recv, device):
        return pltpu.make_async_remote_copy(
            src_ref=src, dst_ref=dst, send_sem=send, recv_sem=recv,
            device_id=device, device_id_type=MESH,
        )

    ints_copy = pltpu.make_async_copy(ints_ref, weights.at[:, xh, pl.ds(0, 256)], local_sem.at[0])
    ints_copy.start()
    t2_copy = pltpu.make_async_copy(t2_ref.at[wide], gathered.at[wide, z, xl], local_sem.at[1])
    t2_copy.start()
    t2_narrow = pltpu.make_async_copy(
        t2_ref.at[narrow], gathered.at[narrow, z, xh], local_sem.at[2]
    )

    @pl.when(outer)
    def _():
        t2_narrow.start()

    barrier = pltpu.get_barrier_semaphore()
    for device in (
        z_dev[0], z_dev[1], x_dev, xh_dev, xd_dev, yp_dev, ym_dev, co_dev, yp_other, ym_other
    ):
        pl.semaphore_signal(barrier, inc=1, device_id=device, device_id_type=MESH)
    pl.semaphore_wait(barrier, 10)

    def x0_copy(s, col):
        return remote(t2_ref.at[s], gathered.at[s, z, col], x0_s.at[s], x0_r.at[s], x_dev)

    def pb_copy(s, i, group):
        return remote(
            t2_ref.at[s], gathered.at[s, z, group], pb_s.at[i, s], pb_r.at[s], (xd_dev, xh_dev)[i]
        )

    def send_rows(s, k):
        @pl.when(outer)
        def _():
            x0_copy(s, xh).start()

        @pl.when(inner)
        def _():
            pb_copy(s, 0, xh).start()
            pb_copy(s, 1, xh).start()

    def w_copy(s):
        return remote(
            ints_ref.at[s], weights.at[s, xh, pl.ds(256, 256)], w_s.at[s], w_r.at[s], co_dev
        )

    def wx_copy(s, group):
        return remote(
            ints_ref.at[s], weights.at[s, group, pl.ds(0, 256)], wx_s.at[s], wx_r.at[s], xh_dev
        )

    def wf_copy(s):
        return remote(
            weights.at[s, 1 - xh, pl.ds(0, 256)], weights.at[s, 1 - xh, pl.ds(256, 256)],
            wf_s.at[s], wf_r.at[s], co_dev,
        )

    def send_weights(s, k):
        wx_copy(s, xh).start()

    def forward_weights(s, k):
        wx_copy(s, 1 - xh).wait_recv()
        wf_copy(s).start()

    def z_copy(s, k, direction, sender_side, is_wide):
        sign = -1 if direction == 0 else 1
        b = zmod(z + sign * (k - 1 if sender_side else k))
        if k < 3 or (k == 3 and not is_wide):
            view = gathered.at[s, b]
        elif k == 3:
            view = gathered.at[s, b, xl]
        elif is_wide:
            view = gathered.at[s, b, xl, pl.ds(32 * direction, 32)]
        else:
            view = gathered.at[s, b, direction]
        return remote(view, view, z_s.at[k - 1, direction, s], z_r.at[k - 1, direction, s], z_dev[direction])

    def z_one(s, direction, sender_side, own):
        b = z if sender_side else zmod(z + (-1 if direction == 0 else 1))
        view = gathered.at[s, b, xl if own else 1 - xl]
        i = 0 if own else 4
        return remote(view, view, z_s.at[i, direction, s], z_r.at[i, direction, s], z_dev[direction])

    def z_send(s, k, is_wide):
        for direction in range(2):
            z_copy(s, k, direction, True, is_wide).start()

    def z_recv(s, k, is_wide):
        for direction in range(2):
            if is_wide and k == 1:
                z_one(s, direction, False, True).wait_recv()
                z_one(s, direction, False, False).wait_recv()
            else:
                z_copy(s, k, direction, False, is_wide).wait_recv()

    def xf_copy(s, f, sender_side):
        col = xl if sender_side else 1 - xl
        view = gathered.at[s, zmod(z + (-3, 3, 4)[f]), col]
        return remote(view, view, xf_s.at[f, s], xf_r.at[f, s], x_dev)

    turn = jnp.where(lax.rem(z, 2) == 0, -1, 1)

    def owner(k):
        own = z // 2
        return ymod((own, own + turn, own - turn, own + 2)[k - 1])

    def buffers(is_wide, s):
        if is_wide:
            return s, partial, full_hi, full_lo, half_hi, half_lo
        return s - WIDE, n_partial, n_full_hi, n_full_lo, n_half_hi, n_half_lo

    def half_copy(s, k, side, is_wide):
        i, part, _, _, hi, lo = buffers(is_wide, s)
        return remote(
            part.at[i, k - 1, side], (hi, lo)[side].at[i], yh_s.at[side, s], yh_r.at[side, s],
            (ym_dev, yp_dev)[side],
        )

    def full_copy(s, k, side, is_wide):
        i, part, hi, lo, _, _ = buffers(is_wide, s)
        return remote(
            part.at[i, k - 1], (hi, lo)[side].at[i], yf_s.at[side, s], yf_r.at[side, s],
            (ym_dev, yp_dev)[side],
        )

    def n_full_copy(s, k, side, other):
        return remote(
            n_partial.at[s - WIDE, k - 1, :, :, pl.ds(256 * other, 256)],
            (n_full_hi, n_full_lo)[side].at[s - WIDE, other],
            yf_s.at[side + 2 * other, s], yf_r.at[side + 2 * other, s],
            ((ym_dev, yp_dev), (ym_other, yp_other))[other][side],
        )

    def n_sib_copy(s, k):
        return remote(
            n_partial.at[s - WIDE, k - 1, :, :, pl.ds(256, 256)], n_sib.at[s - WIDE],
            co_s.at[s], co_r.at[s], co_dev,
        )

    def xh_copy(s):
        return remote(xsend.at[s], xrecv.at[s], xh_s.at[s], xh_r.at[s], xh_dev)

    def co_copy(s, whose):
        return remote(
            sib_send.at[s], result.at[pl.ds(2 * s, 2), :, whose], co_s.at[s], co_r.at[s], co_dev
        )

    def contract(rows, w):
        return lax.dot_general(rows, w, (((1,), (1,)), ((), ())), preferred_element_type=jnp.float32)

    def stage1(s, k, is_wide):
        first = pl.ds(2 * owner(k), 2)
        i, part = buffers(is_wide, s)[:2]
        if is_wide:
            product = contract(gathered[s, first].reshape(4 * ROWS, K), weights[s, xh])
            part[i, k - 1] = product.astype(jnp.bfloat16).reshape(2, 2, ROWS, 512)
        else:
            product = contract(
                gathered[s, first, 0].reshape(2 * ROWS, K), weights[s, 0]
            ) + contract(gathered[s, first, 1].reshape(2 * ROWS, K), weights[s, 1])
            part[i, k - 1] = product.astype(jnp.bfloat16).reshape(2, ROWS, 512)

            @pl.when(y == owner(k))
            def _():
                n_sib_copy(s, k).start()

        @pl.when(ymod(y - owner(k)) == 2)
        def _():
            half_copy(s, k, 0, is_wide).start()
            half_copy(s, k, 1, is_wide).start()

    def stage2(s, k, is_wide):
        i, part, _, _, hi, lo = buffers(is_wide, s)
        d = ymod(y - owner(k))
        for side, role, recv in ((0, 1, hi), (1, 3, lo)):
            @pl.when(d == role)
            def _():
                half_copy(s, k, side, is_wide).wait_recv()
                part[i, k - 1, side] = (
                    part[i, k - 1, side].astype(jnp.float32) + recv[i].astype(jnp.float32)
                ).astype(jnp.bfloat16)
                if is_wide:
                    full_copy(s, k, side, is_wide).start()
                else:
                    n_full_copy(s, k, side, 1).start()
                    n_full_copy(s, k, side, 0).start()

    def three(s, k, col):
        return (
            partial[s, k - 1, :, col].astype(jnp.float32)
            + full_hi[s, :, col].astype(jnp.float32)
            + full_lo[s, :, col].astype(jnp.float32)
        )

    def deliver(s, final):
        for h in range(2):
            sib_send[s, h] = final[:, :, 256 + 128 * h:256 + 128 * (h + 1)]
        co_copy(s, core).start()
        for h in range(2):
            result[2 * s + h, :, core] = final[:, :, 128 * h:128 * (h + 1)]

    def stage3(s, k, is_wide):
        @pl.when(y == owner(k))
        def _():
            if is_wide:
                full_copy(s, k, 0, is_wide).wait_recv()
                full_copy(s, k, 1, is_wide).wait_recv()
                xsend[s] = three(s, k, 1 - xh).astype(jnp.bfloat16)
                xh_copy(s).start()
            else:
                i, part, hi, lo, _, _ = buffers(False, s)
                n_sib_copy(s, k).wait_recv()
                for other in range(2):
                    n_full_copy(s, k, 0, other).wait_recv()
                    n_full_copy(s, k, 1, other).wait_recv()
                    mine = n_sib[i] if other else part[i, k - 1, :, :, 0:256]
                    final = (
                        mine.astype(jnp.float32)
                        + hi[i, other].astype(jnp.float32)
                        + lo[i, other].astype(jnp.float32)
                    ).astype(jnp.bfloat16)
                    for h in range(2):
                        result[2 * s + h, :, 1 - core if other else core] = (
                            final[:, :, 128 * h:128 * (h + 1)]
                        )

    def stage4(s, k, is_wide):
        if is_wide:
            @pl.when(y == owner(k))
            def _():
                xh_copy(s).wait_recv()
                final = three(s, k, xh) + xrecv[s].astype(jnp.float32)
                deliver(s, final.astype(jnp.bfloat16))

    def first(s, k, is_wide):
        if is_wide:
            for direction in range(2):
                z_one(s, direction, True, True).start()

    def begin(s, k, is_wide):
        if is_wide:
            x0_copy(s, 1 - xl).wait_recv()
            for direction in range(2):
                z_one(s, direction, True, False).start()
        else:
            @pl.when(inner)
            def _():
                x0_copy(s, xh).wait_recv()

            pb_copy(s, 0, 1 - xh).wait_recv()
            z_send(s, 1, is_wide)

    def arrive(s, k, is_wide):
        z_recv(s, k, is_wide)
        if k < 4:
            z_send(s, k + 1, is_wide)
        if is_wide and k == 3:
            xf_copy(s, 0, True).start()
            xf_copy(s, 1, True).start()
        if is_wide and k == 4:
            xf_copy(s, 2, True).start()

    def multiply(s, k, is_wide):
        if k == 1:
            w_copy(s).wait_recv()
            if not is_wide:
                wf_copy(s).wait_recv()
        if is_wide and k == 3:
            xf_copy(s, 0, False).wait_recv()
            xf_copy(s, 1, False).wait_recv()
        if is_wide and k == 4:
            xf_copy(s, 2, False).wait_recv()
        stage1(s, k, is_wide)

    def send_own(s, carry):
        x0_copy(s, xl).start()
        w_copy(s).start()
        return carry

    def send_w(s, carry):
        w_copy(s).start()
        return carry

    lax.fori_loop(0, WIDE, send_own, 0)
    lax.fori_loop(WIDE, NSYM, send_w, 0)
    t2_copy.wait()

    for s in range(EARLY):
        first(s, 1, True)

    @pl.when(outer)
    def _():
        t2_narrow.wait()

    ints_copy.wait()

    actions = {
        "first": first, "begin": begin, "arrive": arrive, "multiply": multiply,
        "add": stage2, "own": stage3, "finish": stage4,
    }
    narrow_actions = {
        "rows": send_rows, "weights": send_weights, "forward": forward_weights,
    }

    def within(s, low, high, act):
        @pl.when(jnp.logical_and(s >= low, s < high))
        def _():
            act()

    def tick_body(tick, carry):
        for name, k, back in SCHEDULE:
            s = tick - back
            if name in narrow_actions:
                within(s, WIDE, NSYM, lambda: narrow_actions[name](s, k))
            else:
                within(s, 0, WIDE, lambda: actions[name](s, k, True))
                within(s, WIDE, NSYM, lambda: actions[name](s, k, False))
        return carry

    lax.fori_loop(0, NSYM + max(entry[2] for entry in SCHEDULE), tick_body, 0)

    def drain_common(s, is_wide):
        w_copy(s).wait_send()
        for direction in range(2):
            if is_wide:
                z_one(s, direction, True, True).wait_send()
                z_one(s, direction, True, False).wait_send()
            else:
                z_copy(s, 1, direction, True, is_wide).wait_send()
            for k in range(2, 5):
                z_copy(s, k, direction, True, is_wide).wait_send()
        for side in range(2):
            half_copy(s, 1, side, is_wide).wait_send()
            if is_wide:
                full_copy(s, 1, side, is_wide).wait_send()
            else:
                n_full_copy(s, 1, side, 0).wait_send()
                n_full_copy(s, 1, side, 1).wait_send()
        if is_wide:
            co_copy(s, core).wait_send()
            co_copy(s, 1 - core).wait_recv()
        else:
            n_sib_copy(s, 1).wait_send()

    def drain_wide(s, carry):
        x0_copy(s, xl).wait_send()
        for f in range(3):
            xf_copy(s, f, True).wait_send()
        xh_copy(s).wait_send()
        drain_common(s, True)
        return carry

    def drain_narrow(s, carry):
        @pl.when(outer)
        def _():
            x0_copy(s, xh).wait_send()

        @pl.when(inner)
        def _():
            pb_copy(s, 0, xh).wait_send()
            pb_copy(s, 1, xh).wait_send()

        wx_copy(s, xh).wait_send()
        wf_copy(s).wait_send()
        drain_common(s, False)
        return carry

    lax.fori_loop(0, WIDE, drain_wide, 0)
    lax.fori_loop(WIDE, NSYM, drain_narrow, 0)

    out_copy = pltpu.make_async_copy(result, out_ref, local_sem.at[0])
    out_copy.start()
    out_copy.wait()


def merge_tiles(load, first, second):
    pieces = []
    for want, tile in ((0, first), (1, second)):
        a = load(tile // 2)
        pieces.append(jnp.where(lax.rem(tile, 2) == want, a, pltpu.roll(a, 64, 1)))
    lane = lax.broadcasted_iota(jnp.int32, pieces[0].shape, 1)
    return jnp.where(lane < 64, pieces[0], pieces[1])


def sort_kernel(ab_ref, cd_ref, t2_ref, ints_ref, t2_out, ints_out, inverse_ref, order, count, sem):
    def clear(s, carry):
        count[s] = 0
        count[NSYM + s] = 0
        return carry

    lax.fori_loop(0, NSYM, clear, 0)

    def place_ab(i, carry):
        s = ab_ref[i]
        c = count[NSYM + s]
        inverse_ref[i] = s * 4 + c
        pltpu.make_async_copy(ints_ref.at[i], ints_out.at[s, c], sem).start()
        count[NSYM + s] = c + 1
        return carry

    lax.fori_loop(0, 32, place_ab, 0, unroll=4)
    def place_cd(i, carry):
        s = cd_ref[i]
        c = count[s]
        order[s * 8 + c] = i
        count[s] = c + 1
        return carry

    lax.fori_loop(0, 64, place_cd, 0, unroll=4)

    whole = pltpu.make_async_copy(ints_out, ints_out, sem)

    def load(chunk):
        return t2_ref[:, pl.ds(pl.multiple_of(chunk * 128, 128), 128)]

    def sort_t2(s, carry):
        for j in range(K // 128):
            t2_out[s, :, 128 * j:128 * (j + 1)] = merge_tiles(
                load, order[s * 8 + 2 * j], order[s * 8 + 2 * j + 1]
            )
        return carry

    lax.fori_loop(0, NSYM, sort_t2, 0)
    whole.wait()


def unsort_kernel(inverse_ref, sorted_ref, out_ref):
    for p in range(16):
        out_ref[:, 128 * p:128 * (p + 1)] = merge_tiles(
            lambda chunk: sorted_ref[chunk], inverse_ref[2 * p], inverse_ref[2 * p + 1]
        )


def per_device(t2_amps, integrals, ab_sym, cd_sym):
    bf16 = jnp.bfloat16
    dma = pltpu.SemaphoreType.DMA
    smem = pl.BlockSpec(memory_space=pltpu.SMEM)
    vmem = pl.BlockSpec(memory_space=pltpu.VMEM)
    hbm = pl.BlockSpec(memory_space=pltpu.HBM)
    t2_sorted, ints_sorted, inverse = pl.pallas_call(
        sort_kernel,
        out_shape=(
            jax.ShapeDtypeStruct((NSYM, ROWS, K), bf16),
            jax.ShapeDtypeStruct((NSYM, 4, 64, K), bf16),
            jax.ShapeDtypeStruct((32,), jnp.int32),
        ),
        in_specs=[smem, smem, vmem, hbm],
        out_specs=(vmem, vmem, smem),
        scratch_shapes=[pltpu.SMEM((64,), jnp.int32), pltpu.SMEM((16,), jnp.int32), dma(())],
    )(ab_sym, cd_sym, t2_amps, integrals)
    result = pl.pallas_call(
        kernel,
        out_shape=jax.ShapeDtypeStruct((2 * NSYM, 2, 2, ROWS, 128), bf16),
        in_specs=[hbm, hbm],
        out_specs=hbm,
        scratch_shapes=[
            pltpu.VMEM((NSYM, NZ, 2, ROWS, K), bf16),
            pltpu.VMEM((NSYM, 2, 512, K), bf16),
            pltpu.VMEM((WIDE, 4, 2, 2, ROWS, 512), bf16),
            pltpu.VMEM((WIDE, 2, 2, ROWS, 512), bf16),
            pltpu.VMEM((WIDE, 2, 2, ROWS, 512), bf16),
            pltpu.VMEM((WIDE, 2, ROWS, 512), bf16),
            pltpu.VMEM((WIDE, 2, ROWS, 512), bf16),
            pltpu.VMEM((WIDE, 2, ROWS, 512), bf16),
            pltpu.VMEM((WIDE, 2, ROWS, 512), bf16),
            pltpu.VMEM((NARROW, 4, 2, ROWS, 512), bf16),
            pltpu.VMEM((NARROW, 2, 2, ROWS, 256), bf16),
            pltpu.VMEM((NARROW, 2, 2, ROWS, 256), bf16),
            pltpu.VMEM((NARROW, ROWS, 512), bf16),
            pltpu.VMEM((NARROW, ROWS, 512), bf16),
            pltpu.VMEM((NARROW, 2, ROWS, 256), bf16),
            pltpu.VMEM((NSYM, 2, 2, ROWS, 128), bf16),
            pltpu.VMEM((2 * NSYM, 2, 2, ROWS, 128), bf16),
            dma((3,)),
            dma((NSYM,)), dma((NSYM,)),
            dma((NSYM,)), dma((NSYM,)),
            dma((5, 2, NSYM)), dma((5, 2, NSYM)),
            dma((3, NSYM)), dma((3, NSYM)),
            dma((2, NSYM)), dma((2, NSYM)),
            dma((4, NSYM)), dma((4, NSYM)),
            dma((NSYM,)), dma((NSYM,)),
            dma((NSYM,)), dma((NSYM,)),
            dma((NSYM,)), dma((NSYM,)),
            dma((NSYM,)), dma((NSYM,)),
            dma((2, NSYM)), dma((NSYM,)),
        ],
        compiler_params=pltpu.CompilerParams(
            collective_id=0, has_side_effects=True, vmem_limit_bytes=62 << 20
        ),
    )(t2_sorted, ints_sorted.reshape(NSYM, 256, K))
    return pl.pallas_call(
        unsort_kernel,
        out_shape=jax.ShapeDtypeStruct((256, 2048), bf16),
        in_specs=[smem, vmem],
        out_specs=vmem,
    )(inverse, result.reshape(2 * NSYM, 256, 128))


def solution(mesh):
    in_specs = (P("blk", "cd"), P("blk", None, "cd"), P("blk"), P("cd"))
    out_specs = P("cd", "blk")
    return jax.shard_map(
        per_device, mesh=mesh, in_specs=in_specs, out_specs=out_specs, check_vma=False
    )
```

```python
import jax
import jax.numpy as jnp
from jax import lax
from jax.experimental import pallas as pl
from jax.experimental.pallas import tpu as pltpu
from jax.sharding import PartitionSpec as P

MESH = pl.DeviceIdType.MESH
NSYM = 8
NZ = 8
NY = 4
ROWS = 64
K = 512
WIDE = 6
NARROW = NSYM - WIDE
EARLY = 2
SCHEDULE = (
    ("begin", 0, 0),
    ("finish", 4, 6),
    ("own", 4, 5),
    ("arrive", 2, 1),
    ("add", 2, 2),
    ("multiply", 2, 1),
    ("add", 3, 3),
    ("arrive", 4, 2),
    ("multiply", 3, 2),
    ("finish", 2, 4),
    ("own", 2, 3),
    ("forward", 0, -2),
    ("arrive", 1, 0),
    ("rows", 0, -6),
    ("finish", 3, 5),
    ("own", 3, 4),
    ("add", 1, 1),
    ("multiply", 1, 0),
    ("arrive", 3, 1),
    ("weights", 0, -6),
    ("finish", 1, 3),
    ("own", 1, 2),
    ("first", 1, -2),
    ("add", 4, 3),
    ("multiply", 4, 2),
)


def kernel(
    t2_ref, ints_ref, out_ref,
    gathered, weights, partial, full_hi, full_lo, half_hi, half_lo, xsend, xrecv,
    n_partial, n_full_hi, n_full_lo, n_half_hi, n_half_lo, n_sib, sib_send, result,
    local_sem, w_s, w_r, x0_s, x0_r, z_s, z_r, xf_s, xf_r, yh_s, yh_r, yf_s, yf_r, xh_s, xh_r,
    co_s, co_r, wx_s, wx_r, wf_s, wf_r, pb_s, pb_r,
):
    blk = lax.axis_index("blk")
    cd = lax.axis_index("cd")
    core = lax.rem(blk, 2)
    z = lax.rem(blk // 2, NZ)
    xl = blk // (2 * NZ)
    y = lax.rem(cd, NY)
    xh = cd // NY

    def dev(xl_, z_, core_, xh_, y_):
        return ((xl_ * NZ + z_) * 2 + core_, xh_ * NY + y_)

    def zmod(v):
        return lax.rem(v + 2 * NZ, NZ)

    def ymod(v):
        return lax.rem(v + 2 * NY, NY)

    z_dev = (dev(xl, zmod(z + 1), core, xh, y), dev(xl, zmod(z - 1), core, xh, y))
    x_dev = dev(1 - xl, z, core, xh, y)
    xh_dev = dev(xl, z, core, 1 - xh, y)
    xd_dev = dev(1 - xl, z, core, 1 - xh, y)
    yp_dev = dev(xl, z, core, xh, ymod(y + 1))
    ym_dev = dev(xl, z, core, xh, ymod(y - 1))
    co_dev = dev(xl, z, 1 - core, xh, y)
    yp_other = dev(xl, z, 1 - core, xh, ymod(y + 1))
    ym_other = dev(xl, z, 1 - core, xh, ymod(y - 1))
    outer = xl == xh
    inner = jnp.logical_not(outer)
    wide, narrow = pl.ds(0, WIDE), pl.ds(WIDE, NARROW)

    def remote(src, dst, send, recv, device):
        return pltpu.make_async_remote_copy(
            src_ref=src, dst_ref=dst, send_sem=send, recv_sem=recv,
            device_id=device, device_id_type=MESH,
        )

    ints_copy = pltpu.make_async_copy(ints_ref, weights.at[:, xh, pl.ds(0, 256)], local_sem.at[0])
    ints_copy.start()
    t2_copy = pltpu.make_async_copy(t2_ref.at[wide], gathered.at[wide, z, xl], local_sem.at[1])
    t2_copy.start()
    t2_narrow = pltpu.make_async_copy(
        t2_ref.at[narrow], gathered.at[narrow, z, xh], local_sem.at[2]
    )

    @pl.when(outer)
    def _():
        t2_narrow.start()

    barrier = pltpu.get_barrier_semaphore()
    for device in (
        z_dev[0], z_dev[1], x_dev, xh_dev, xd_dev, yp_dev, ym_dev, co_dev, yp_other, ym_other
    ):
        pl.semaphore_signal(barrier, inc=1, device_id=device, device_id_type=MESH)
    pl.semaphore_wait(barrier, 10)

    def x0_copy(s, col):
        return remote(t2_ref.at[s], gathered.at[s, z, col], x0_s.at[s], x0_r.at[s], x_dev)

    def pb_copy(s, i, group):
        return remote(
            t2_ref.at[s], gathered.at[s, z, group], pb_s.at[i, s], pb_r.at[s], (xd_dev, xh_dev)[i]
        )

    def send_rows(s, k):
        @pl.when(outer)
        def _():
            x0_copy(s, xh).start()

        @pl.when(inner)
        def _():
            pb_copy(s, 0, xh).start()
            pb_copy(s, 1, xh).start()

    def w_copy(s):
        return remote(
            ints_ref.at[s], weights.at[s, xh, pl.ds(256, 256)], w_s.at[s], w_r.at[s], co_dev
        )

    def wx_copy(s, group):
        return remote(
            ints_ref.at[s], weights.at[s, group, pl.ds(0, 256)], wx_s.at[s], wx_r.at[s], xh_dev
        )

    def wf_copy(s):
        return remote(
            weights.at[s, 1 - xh, pl.ds(0, 256)], weights.at[s, 1 - xh, pl.ds(256, 256)],
            wf_s.at[s], wf_r.at[s], co_dev,
        )

    def send_weights(s, k):
        wx_copy(s, xh).start()

    def forward_weights(s, k):
        wx_copy(s, 1 - xh).wait_recv()
        wf_copy(s).start()

    def z_copy(s, k, direction, sender_side, is_wide):
        sign = -1 if direction == 0 else 1
        b = zmod(z + sign * (k - 1 if sender_side else k))
        if k < 3 or (k == 3 and not is_wide):
            view = gathered.at[s, b]
        elif k == 3:
            view = gathered.at[s, b, xl]
        elif is_wide:
            view = gathered.at[s, b, xl, pl.ds(32 * direction, 32)]
        else:
            view = gathered.at[s, b, direction]
        return remote(view, view, z_s.at[k - 1, direction, s], z_r.at[k - 1, direction, s], z_dev[direction])

    def z_one(s, direction, sender_side, own):
        b = z if sender_side else zmod(z + (-1 if direction == 0 else 1))
        view = gathered.at[s, b, xl if own else 1 - xl]
        i = 0 if own else 4
        return remote(view, view, z_s.at[i, direction, s], z_r.at[i, direction, s], z_dev[direction])

    def z_send(s, k, is_wide):
        for direction in range(2):
            z_copy(s, k, direction, True, is_wide).start()

    def z_recv(s, k, is_wide):
        for direction in range(2):
            if is_wide and k == 1:
                z_one(s, direction, False, True).wait_recv()
                z_one(s, direction, False, False).wait_recv()
            else:
                z_copy(s, k, direction, False, is_wide).wait_recv()

    def xf_copy(s, f, sender_side):
        col = xl if sender_side else 1 - xl
        view = gathered.at[s, zmod(z + (-3, 3, 4)[f]), col]
        return remote(view, view, xf_s.at[f, s], xf_r.at[f, s], x_dev)

    turn = jnp.where(lax.rem(z, 2) == 0, -1, 1)

    def owner(k):
        own = z // 2
        return ymod((own, own + turn, own - turn, own + 2)[k - 1])

    def buffers(is_wide, s):
        if is_wide:
            return s, partial, full_hi, full_lo, half_hi, half_lo
        return s - WIDE, n_partial, n_full_hi, n_full_lo, n_half_hi, n_half_lo

    def half_copy(s, k, side, is_wide):
        i, part, _, _, hi, lo = buffers(is_wide, s)
        return remote(
            part.at[i, k - 1, side], (hi, lo)[side].at[i], yh_s.at[side, s], yh_r.at[side, s],
            (ym_dev, yp_dev)[side],
        )

    def full_copy(s, k, side, is_wide):
        i, part, hi, lo, _, _ = buffers(is_wide, s)
        return remote(
            part.at[i, k - 1], (hi, lo)[side].at[i], yf_s.at[side, s], yf_r.at[side, s],
            (ym_dev, yp_dev)[side],
        )

    def n_full_copy(s, k, side, other):
        return remote(
            n_partial.at[s - WIDE, k - 1, :, :, pl.ds(256 * other, 256)],
            (n_full_hi, n_full_lo)[side].at[s - WIDE, other],
            yf_s.at[side + 2 * other, s], yf_r.at[side + 2 * other, s],
            ((ym_dev, yp_dev), (ym_other, yp_other))[other][side],
        )

    def n_sib_copy(s, k):
        return remote(
            n_partial.at[s - WIDE, k - 1, :, :, pl.ds(256, 256)], n_sib.at[s - WIDE],
            co_s.at[s], co_r.at[s], co_dev,
        )

    def xh_copy(s):
        return remote(xsend.at[s], xrecv.at[s], xh_s.at[s], xh_r.at[s], xh_dev)

    def co_copy(s, whose):
        return remote(
            sib_send.at[s], result.at[pl.ds(2 * s, 2), :, whose], co_s.at[s], co_r.at[s], co_dev
        )

    def contract(rows, w):
        return lax.dot_general(rows, w, (((1,), (1,)), ((), ())), preferred_element_type=jnp.float32)

    def stage1(s, k, is_wide):
        first = pl.ds(2 * owner(k), 2)
        i, part = buffers(is_wide, s)[:2]
        if is_wide:
            product = contract(gathered[s, first].reshape(4 * ROWS, K), weights[s, xh])
            part[i, k - 1] = product.astype(jnp.bfloat16).reshape(2, 2, ROWS, 512)
        else:
            product = contract(
                gathered[s, first, 0].reshape(2 * ROWS, K), weights[s, 0]
            ) + contract(gathered[s, first, 1].reshape(2 * ROWS, K), weights[s, 1])
            part[i, k - 1] = product.astype(jnp.bfloat16).reshape(2, ROWS, 512)

            @pl.when(y == owner(k))
            def _():
                n_sib_copy(s, k).start()

        @pl.when(ymod(y - owner(k)) == 2)
        def _():
            half_copy(s, k, 0, is_wide).start()
            half_copy(s, k, 1, is_wide).start()

    def stage2(s, k, is_wide):
        i, part, _, _, hi, lo = buffers(is_wide, s)
        d = ymod(y - owner(k))
        for side, role, recv in ((0, 1, hi), (1, 3, lo)):
            @pl.when(d == role)
            def _():
                half_copy(s, k, side, is_wide).wait_recv()
                part[i, k - 1, side] = (
                    part[i, k - 1, side].astype(jnp.float32) + recv[i].astype(jnp.float32)
                ).astype(jnp.bfloat16)
                if is_wide:
                    full_copy(s, k, side, is_wide).start()
                else:
                    n_full_copy(s, k, side, 1).start()
                    n_full_copy(s, k, side, 0).start()

    def three(s, k, col):
        return (
            partial[s, k - 1, :, col].astype(jnp.float32)
            + full_hi[s, :, col].astype(jnp.float32)
            + full_lo[s, :, col].astype(jnp.float32)
        )

    def deliver(s, final):
        for h in range(2):
            sib_send[s, h] = final[:, :, 256 + 128 * h:256 + 128 * (h + 1)]
        co_copy(s, core).start()
        for h in range(2):
            result[2 * s + h, :, core] = final[:, :, 128 * h:128 * (h + 1)]

    def stage3(s, k, is_wide):
        @pl.when(y == owner(k))
        def _():
            if is_wide:
                full_copy(s, k, 0, is_wide).wait_recv()
                full_copy(s, k, 1, is_wide).wait_recv()
                xsend[s] = three(s, k, 1 - xh).astype(jnp.bfloat16)
                xh_copy(s).start()
            else:
                i, part, hi, lo, _, _ = buffers(False, s)
                n_sib_copy(s, k).wait_recv()
                for other in range(2):
                    n_full_copy(s, k, 0, other).wait_recv()
                    n_full_copy(s, k, 1, other).wait_recv()
                    mine = n_sib[i] if other else part[i, k - 1, :, :, 0:256]
                    final = (
                        mine.astype(jnp.float32)
                        + hi[i, other].astype(jnp.float32)
                        + lo[i, other].astype(jnp.float32)
                    ).astype(jnp.bfloat16)
                    for h in range(2):
                        result[2 * s + h, :, 1 - core if other else core] = (
                            final[:, :, 128 * h:128 * (h + 1)]
                        )

    def stage4(s, k, is_wide):
        if is_wide:
            @pl.when(y == owner(k))
            def _():
                xh_copy(s).wait_recv()
                final = three(s, k, xh) + xrecv[s].astype(jnp.float32)
                deliver(s, final.astype(jnp.bfloat16))

    def first(s, k, is_wide):
        if is_wide:
            for direction in range(2):
                z_one(s, direction, True, True).start()

    def begin(s, k, is_wide):
        if is_wide:
            x0_copy(s, 1 - xl).wait_recv()
            for direction in range(2):
                z_one(s, direction, True, False).start()
        else:
            @pl.when(inner)
            def _():
                x0_copy(s, xh).wait_recv()

            pb_copy(s, 0, 1 - xh).wait_recv()
            z_send(s, 1, is_wide)

    def arrive(s, k, is_wide):
        z_recv(s, k, is_wide)
        if k < 4:
            z_send(s, k + 1, is_wide)
        if is_wide and k == 3:
            xf_copy(s, 0, True).start()
            xf_copy(s, 1, True).start()
        if is_wide and k == 4:
            xf_copy(s, 2, True).start()

    def multiply(s, k, is_wide):
        if k == 1:
            w_copy(s).wait_recv()
            if not is_wide:
                wf_copy(s).wait_recv()
        if is_wide and k == 3:
            xf_copy(s, 0, False).wait_recv()
            xf_copy(s, 1, False).wait_recv()
        if is_wide and k == 4:
            xf_copy(s, 2, False).wait_recv()
        stage1(s, k, is_wide)

    def send_own(s, carry):
        x0_copy(s, xl).start()
        w_copy(s).start()
        return carry

    def send_w(s, carry):
        w_copy(s).start()
        return carry

    lax.fori_loop(0, WIDE, send_own, 0)
    lax.fori_loop(WIDE, NSYM, send_w, 0)
    t2_copy.wait()

    for s in range(EARLY):
        first(s, 1, True)

    @pl.when(outer)
    def _():
        t2_narrow.wait()

    ints_copy.wait()

    actions = {
        "first": first, "begin": begin, "arrive": arrive, "multiply": multiply,
        "add": stage2, "own": stage3, "finish": stage4,
    }
    narrow_actions = {
        "rows": send_rows, "weights": send_weights, "forward": forward_weights,
    }

    def within(s, low, high, act):
        @pl.when(jnp.logical_and(s >= low, s < high))
        def _():
            act()

    def drain_common(s, is_wide):
        w_copy(s).wait_send()
        for direction in range(2):
            if is_wide:
                z_one(s, direction, True, True).wait_send()
                z_one(s, direction, True, False).wait_send()
            else:
                z_copy(s, 1, direction, True, is_wide).wait_send()
            for k in range(2, 5):
                z_copy(s, k, direction, True, is_wide).wait_send()
        for side in range(2):
            half_copy(s, 1, side, is_wide).wait_send()
            if is_wide:
                full_copy(s, 1, side, is_wide).wait_send()
            else:
                n_full_copy(s, 1, side, 0).wait_send()
                n_full_copy(s, 1, side, 1).wait_send()
        if is_wide:
            co_copy(s, core).wait_send()
        else:
            n_sib_copy(s, 1).wait_send()

    def drain_wide(s):
        x0_copy(s, xl).wait_send()
        for f in range(3):
            xf_copy(s, f, True).wait_send()
        xh_copy(s).wait_send()
        drain_common(s, True)

    def drain_narrow(s):
        @pl.when(outer)
        def _():
            x0_copy(s, xh).wait_send()

        @pl.when(inner)
        def _():
            pb_copy(s, 0, xh).wait_send()
            pb_copy(s, 1, xh).wait_send()

        wx_copy(s, xh).wait_send()
        wf_copy(s).wait_send()
        drain_common(s, False)

    def out_copy(s):
        part = pl.ds(2 * s, 2)
        return pltpu.make_async_copy(result.at[part], out_ref.at[part], local_sem.at[3 + s])

    def write_out(s):
        co_copy(s, 1 - core).wait_recv()
        out_copy(s).start()

    def tick_body(tick, carry):
        for name, k, back in SCHEDULE:
            s = tick - back
            if name in narrow_actions:
                within(s, WIDE, NSYM, lambda: narrow_actions[name](s, k))
            else:
                within(s, 0, WIDE, lambda: actions[name](s, k, True))
                within(s, WIDE, NSYM, lambda: actions[name](s, k, False))
        within(tick - last, 0, WIDE, lambda: drain_wide(tick - last))
        within(tick - last, WIDE, NSYM, lambda: drain_narrow(tick - last))
        within(tick - last - 1, 0, WIDE, lambda: write_out(tick - last - 1))
        return carry

    last = max(entry[2] for entry in SCHEDULE)

    lax.fori_loop(0, NSYM + last, tick_body, 0)

    for s in range(WIDE, NSYM):
        out_copy(s).start()
    for s in range(NSYM):
        out_copy(s).wait()


def merge_tiles(load, first, second):
    pieces = []
    for want, tile in ((0, first), (1, second)):
        a = load(tile // 2)
        pieces.append(jnp.where(lax.rem(tile, 2) == want, a, pltpu.roll(a, 64, 1)))
    lane = lax.broadcasted_iota(jnp.int32, pieces[0].shape, 1)
    return jnp.where(lane < 64, pieces[0], pieces[1])


def sort_kernel(ab_ref, cd_ref, t2_ref, ints_ref, t2_out, ints_out, inverse_ref, order, count, sem):
    def clear(s, carry):
        count[s] = 0
        count[NSYM + s] = 0
        return carry

    lax.fori_loop(0, NSYM, clear, 0)

    def place_ab(i, carry):
        s = ab_ref[i]
        c = count[NSYM + s]
        inverse_ref[i] = s * 4 + c
        pltpu.make_async_copy(ints_ref.at[i], ints_out.at[s, c], sem).start()
        count[NSYM + s] = c + 1
        return carry

    lax.fori_loop(0, 32, place_ab, 0, unroll=4)
    def place_cd(i, carry):
        s = cd_ref[i]
        c = count[s]
        order[s * 8 + c] = i
        count[s] = c + 1
        return carry

    lax.fori_loop(0, 64, place_cd, 0, unroll=4)

    whole = pltpu.make_async_copy(ints_out, ints_out, sem)

    def load(chunk):
        return t2_ref[:, pl.ds(pl.multiple_of(chunk * 128, 128), 128)]

    def sort_t2(s, carry):
        for j in range(K // 128):
            t2_out[s, :, 128 * j:128 * (j + 1)] = merge_tiles(
                load, order[s * 8 + 2 * j], order[s * 8 + 2 * j + 1]
            )
        return carry

    lax.fori_loop(0, NSYM, sort_t2, 0)
    whole.wait()


def unsort_kernel(inverse_ref, sorted_ref, out_ref):
    for p in range(16):
        out_ref[:, 128 * p:128 * (p + 1)] = merge_tiles(
            lambda chunk: sorted_ref[chunk], inverse_ref[2 * p], inverse_ref[2 * p + 1]
        )


def per_device(t2_amps, integrals, ab_sym, cd_sym):
    bf16 = jnp.bfloat16
    dma = pltpu.SemaphoreType.DMA
    smem = pl.BlockSpec(memory_space=pltpu.SMEM)
    vmem = pl.BlockSpec(memory_space=pltpu.VMEM)
    hbm = pl.BlockSpec(memory_space=pltpu.HBM)
    t2_sorted, ints_sorted, inverse = pl.pallas_call(
        sort_kernel,
        out_shape=(
            jax.ShapeDtypeStruct((NSYM, ROWS, K), bf16),
            jax.ShapeDtypeStruct((NSYM, 4, 64, K), bf16),
            jax.ShapeDtypeStruct((32,), jnp.int32),
        ),
        in_specs=[smem, smem, vmem, hbm],
        out_specs=(vmem, vmem, smem),
        scratch_shapes=[pltpu.SMEM((64,), jnp.int32), pltpu.SMEM((16,), jnp.int32), dma(())],
    )(ab_sym, cd_sym, t2_amps, integrals)
    result = pl.pallas_call(
        kernel,
        out_shape=jax.ShapeDtypeStruct((2 * NSYM, 2, 2, ROWS, 128), bf16),
        in_specs=[hbm, hbm],
        out_specs=hbm,
        scratch_shapes=[
            pltpu.VMEM((NSYM, NZ, 2, ROWS, K), bf16),
            pltpu.VMEM((NSYM, 2, 512, K), bf16),
            pltpu.VMEM((WIDE, 4, 2, 2, ROWS, 512), bf16),
            pltpu.VMEM((WIDE, 2, 2, ROWS, 512), bf16),
            pltpu.VMEM((WIDE, 2, 2, ROWS, 512), bf16),
            pltpu.VMEM((WIDE, 2, ROWS, 512), bf16),
            pltpu.VMEM((WIDE, 2, ROWS, 512), bf16),
            pltpu.VMEM((WIDE, 2, ROWS, 512), bf16),
            pltpu.VMEM((WIDE, 2, ROWS, 512), bf16),
            pltpu.VMEM((NARROW, 4, 2, ROWS, 512), bf16),
            pltpu.VMEM((NARROW, 2, 2, ROWS, 256), bf16),
            pltpu.VMEM((NARROW, 2, 2, ROWS, 256), bf16),
            pltpu.VMEM((NARROW, ROWS, 512), bf16),
            pltpu.VMEM((NARROW, ROWS, 512), bf16),
            pltpu.VMEM((NARROW, 2, ROWS, 256), bf16),
            pltpu.VMEM((NSYM, 2, 2, ROWS, 128), bf16),
            pltpu.VMEM((2 * NSYM, 2, 2, ROWS, 128), bf16),
            dma((3 + NSYM,)),
            dma((NSYM,)), dma((NSYM,)),
            dma((NSYM,)), dma((NSYM,)),
            dma((5, 2, NSYM)), dma((5, 2, NSYM)),
            dma((3, NSYM)), dma((3, NSYM)),
            dma((2, NSYM)), dma((2, NSYM)),
            dma((4, NSYM)), dma((4, NSYM)),
            dma((NSYM,)), dma((NSYM,)),
            dma((NSYM,)), dma((NSYM,)),
            dma((NSYM,)), dma((NSYM,)),
            dma((NSYM,)), dma((NSYM,)),
            dma((2, NSYM)), dma((NSYM,)),
        ],
        compiler_params=pltpu.CompilerParams(
            collective_id=0, has_side_effects=True, vmem_limit_bytes=62 << 20
        ),
    )(t2_sorted, ints_sorted.reshape(NSYM, 256, K))
    return pl.pallas_call(
        unsort_kernel,
        out_shape=jax.ShapeDtypeStruct((256, 2048), bf16),
        in_specs=[smem, vmem],
        out_specs=vmem,
    )(inverse, result.reshape(2 * NSYM, 256, 128))


def solution(mesh):
    in_specs = (P("blk", "cd"), P("blk", None, "cd"), P("blk"), P("cd"))
    out_specs = P("cd", "blk")
    return jax.shard_map(
        per_device, mesh=mesh, in_specs=in_specs, out_specs=out_specs, check_vma=False
    )
```
